256 devices in a mesh: lx: 8 (over z), ly: 8 (over x, y_lo), blk: 4 (over y_hi, core).
Axes of the slice: x: 4, y: 4 (y_hi: 2, y_lo: 2; y = y_hi * 2 + y_lo), z: 8, core: 2. Of those that a mesh axis runs over, the one named last changes fastest.
Arguments:
- block_vectors: float32 [32, 1024, 2048], P('blk', 'lx', 'ly'), may hold values from -6 to 6
- search_vectors: float32 [256, 1024, 2048], P('blk', 'lx', 'ly'), may hold values from -6 to 6
- onsite_energy: float32 [1024, 2048], P('lx', 'ly'), may hold values from -1 to 1
- site_mask: int32 [1024, 2048], P('lx', 'ly'), may hold values 0 or 1
- filter_coefs: float32 [5], replicated, may hold values from -1 to 1
Outputs:
- projected: float32 [2, 32, 256], P(None, None, 'blk')
The draws below stay inside these ranges and needn't reach their ends.
Inputs may be any that keep to these rules, and one draw needn't show every extreme that they name: `site_mask`: 1 marks a present site, 0 a vacancy.
All inputs are finite; a program needn't handle non-finite values. No bound on the sum of `site_mask` on one device may be relied on, other than what follows from the above.
Results may differ from the reference program's by a relative error of at most 0.00016.
Values sent between devices are 32-bit elements; how exact they have to be, the bound alone decides.
No kernel may reach another device: no remote copies, remote signals or barrier semaphores. Data moves between devices by JAX's collectives and lax.ppermute only.
A program may use at most 64 MiB of HBM per device.

```python
import math
import jax
import jax.numpy as jnp
from jax import lax

NV = 256
NB = 32
DEGREE = 4
GX = 1024
GY = 2048


def with_ends(drawn, stream_key, low, high):
    longest = drawn.shape.index(max(drawn.shape))
    spots = []
    for shift in (0, 1):
        where = [jax.random.randint(jax.random.fold_in(stream_key, axis), (), 0, length) for axis, length in enumerate(drawn.shape)]
        where[longest] = (where[longest] + shift) % drawn.shape[longest]
        spots.append(tuple(where))
    return drawn.at[spots[0]].set(low).at[spots[1]].set(high)


def levels(rng, shape, cuts, smallest, largest):
    gain, own = 1.0, jax.random.fold_in(rng, 6)
    for position, blocks in cuts:
        steps = jnp.exp(jax.random.uniform(jax.random.fold_in(own, position), (blocks,), jnp.float32, smallest / len(cuts), largest / len(cuts)))
        gain = gain * jnp.repeat(steps, shape[position] // blocks).reshape([-1 if axis == position else 1 for axis in range(len(shape))])
    return gain


def centred(stream_key, extent, scale, reach, cuts=(), held_as=jnp.bfloat16):
    entries = scale * jax.random.normal(stream_key, extent, jnp.float32)
    if cuts:
        entries = entries * levels(stream_key, extent, cuts, -0.22, 0.18)
    return jnp.clip(entries, -reach, reach).astype(held_as)


def setup_inputs(seed: int = 0) -> dict:
    key_of = jax.random.split(jax.random.key(seed), 6)
    block_vectors = centred(key_of[0], (NB, GX, GY), 1.0, 6.0, ((0, 4), (1, 8), (2, 8)), jnp.float32)
    search_vectors = centred(key_of[1], (NV, GX, GY), 1.0, 6.0, ((0, 4), (1, 8), (2, 8)), jnp.float32)
    onsite_energy = jnp.clip(jax.random.uniform(key_of[2], (GX, GY), jnp.float32, -1.0, 1.0) * levels(key_of[2], (GX, GY), ((0, 8), (1, 8)), -0.4, 0.0), -1.0, 1.0)
    site_mask = with_ends((jax.random.randint(key_of[3], (GX, GY), 0, 20) < 19).astype(jnp.int32), jax.random.fold_in(key_of[3], 1), 0, 1)
    filter_coefs = jnp.clip(jax.random.uniform(key_of[4], (DEGREE + 1,), jnp.float32, -1.0, 1.0), -1.0, 1.0)
    return {"block_vectors": block_vectors, "search_vectors": search_vectors, "onsite_energy": onsite_energy, "site_mask": site_mask, "filter_coefs": filter_coefs}


def scaled_step(padded, onsite, present):
    nrows, ncols = onsite.shape
    row_index = lax.broadcasted_iota(jnp.int32, (nrows, ncols), 0)
    col_index = lax.broadcasted_iota(jnp.int32, (nrows, ncols), 1)
    even_sites = (row_index + col_index) % 2 == 0
    centre = padded[..., 1:-1, 1:-1]
    left_side = padded[..., 1:-1, :-2]
    right_side = padded[..., 1:-1, 2:]
    upper_side = padded[..., :-2, 1:-1]
    lower_side = padded[..., 2:, 1:-1]
    vertical = jnp.where(even_sites, lower_side, upper_side)
    return present * (onsite * centre - (left_side + right_side + vertical)) * 0.25

def border(field):
    return jnp.pad(field, ((0, 0), (1, 1), (1, 1)))

def reference(block_vectors, search_vectors, onsite_energy, site_mask, filter_coefs):
    present = site_mask.astype(jnp.float32)
    current = block_vectors * present
    filtered = filter_coefs[0] * current
    before = current
    for order in range(1, DEGREE + 1):
        image = scaled_step(border(current), onsite_energy, present)
        following = image if order == 1 else 2.0 * image - before
        before, current = (current, following)
        filtered = filtered + filter_coefs[order] * current
    image = scaled_step(border(filtered), onsite_energy, present)
    stacked = jnp.stack([filtered, image]).reshape(2 * NB, GX * GY)
    search_flat = search_vectors.reshape(NV, GX * GY)
    gram = lax.dot_general(stacked, search_flat, (((1,), (1,)), ((), ())), precision=lax.Precision.HIGHEST, preferred_element_type=jnp.float32)
    scale_factor = 1.0 / math.sqrt(GX * GY)
    return (gram * scale_factor).reshape(2, NB, NV)
```

```python
import math

import jax
import jax.numpy as jnp
from jax import lax
from jax.sharding import PartitionSpec as P


def extended(block, sides, width):
    for axis, dim in sides:
        count = lax.axis_size(axis)
        forward = [(i, i + 1) for i in range(count - 1)]
        backward = [(target, source) for source, target in forward]
        low = lax.ppermute(
            lax.slice_in_dim(block, block.shape[dim] - width, None, axis=dim), axis, forward
        )
        high = lax.ppermute(lax.slice_in_dim(block, 0, width, axis=dim), axis, backward)
        block = jnp.concatenate([low, block, high], axis=dim)
    return block


def scaled_step(padded, onsite, present):
    nrows, ncols = onsite.shape
    row_index = lax.broadcasted_iota(jnp.int32, (nrows, ncols), 0)
    col_index = lax.broadcasted_iota(jnp.int32, (nrows, ncols), 1)
    even_sites = (row_index + col_index) % 2 == 0
    centre = padded[..., 1:-1, 1:-1]
    left_side = padded[..., 1:-1, :-2]
    right_side = padded[..., 1:-1, 2:]
    upper_side = padded[..., :-2, 1:-1]
    lower_side = padded[..., 2:, 1:-1]
    vertical = jnp.where(even_sites, lower_side, upper_side)
    return present * (onsite * centre - (left_side + right_side + vertical)) * 0.25


def gram_rows(stacked, search_vectors):
    stacks, members, nrows, ncols = stacked.shape
    flat = stacked.reshape(stacks * members, nrows * ncols)
    search_flat = search_vectors.reshape(search_vectors.shape[0], nrows * ncols)
    result = lax.dot_general(
        flat,
        search_flat,
        (((1,), (1,)), ((), ())),
        precision=lax.Precision.HIGH,
        preferred_element_type=jnp.float32,
    )
    return result.reshape(stacks, members, search_vectors.shape[0])


def gathered(paired):
    far = lax.ppermute(paired, "blk", [(0, 2), (1, 3), (2, 0), (3, 1)])
    swap = [(0, 1), (1, 0), (2, 3), (3, 2)]
    near = lax.ppermute(paired, "blk", swap)
    far_near = lax.ppermute(far, "blk", swap)
    return jnp.concatenate([paired, near, far, far_near], axis=1)


def copies_sum(partial, axis):
    count = lax.axis_size(axis)
    copies = jnp.broadcast_to(partial[None], (count,) + partial.shape)
    return lax.all_to_all(copies, axis, 0, 0).sum(0)


def shards(block_vectors, search_vectors, onsite_energy, site_mask, filter_coefs):
    present = site_mask.astype(jnp.float32)
    current = block_vectors * present
    filtered = filter_coefs[0] * current
    degree = filter_coefs.shape[0] - 1
    before = current
    for order in range(1, degree + 1):
        padded_field = extended(current, (("lx", 1), ("ly", 2)), 1)
        image = scaled_step(padded_field, onsite_energy, present)
        following = image if order == 1 else 2.0 * image - before
        before, current = (current, following)
        filtered = filtered + filter_coefs[order] * current
    nrows, ncols = onsite_energy.shape
    scale_factor = 1.0 / math.sqrt(nrows * ncols * lax.axis_size("lx") * lax.axis_size("ly"))
    padded_field = extended(filtered, (("lx", 1), ("ly", 2)), 1)
    image = scaled_step(padded_field, onsite_energy, present)
    paired = jnp.stack([filtered, image])
    partial_gram = gram_rows(gathered(paired), search_vectors).reshape(32, 128)
    total = copies_sum(copies_sum(partial_gram, "ly"), "lx").reshape(2, 4, 8, 64)
    block = lax.axis_index("blk")
    total = jnp.where(block % 2 == 1, total[:, jnp.array([1, 0, 3, 2])], total)
    total = jnp.where(block >= 2, total[:, jnp.array([2, 3, 0, 1])], total)
    return total.reshape(2, 32, 64) * scale_factor


def solution(mesh):
    placed = (P("blk", "lx", "ly"), P("blk", "lx", "ly"), P("lx", "ly"), P("lx", "ly"), P())
    return jax.shard_map(
        shards, mesh=mesh, in_specs=placed, out_specs=P(None, None, "blk"), check_vma=False
    )
```

```python
import math

import jax
import jax.numpy as jnp
from jax import lax
from jax.experimental import pallas as pl
from jax.experimental.pallas import tpu as pltpu
from jax.sharding import PartitionSpec as P

VECS, ROWS, COLS = 8, 128, 256
TILES = ROWS // 8
WIDE = COLS + 128
TOP = 4
EXT = ROWS + 2 * TOP
REACH = 3
GROUP = 8
STRIP = 12
VMEM = pl.BlockSpec(memory_space=pltpu.VMEM)
SMEM = pl.BlockSpec(memory_space=pltpu.SMEM)


def lanes(rows):
    return lax.broadcasted_iota(jnp.int32, (rows, 128), 1)


def packed(tile_of, offset, turn):
    slot = lanes(8) // GROUP
    out = jnp.zeros((8, 128), jnp.float32)
    for t in range(TILES):
        target = (t + turn) % TILES
        moved = pltpu.roll(tile_of(t), (GROUP * target - offset) % 128, 1)
        out = jnp.where(slot == target, moved, out)
    return out


def edges_kernel(v_ref, onsite_ref, mask_ref, left_ref, right_ref, up_ref, down_ref):
    def present(rows, cols):
        return mask_ref[rows, cols].astype(jnp.float32)

    def vector(a, carry):
        def tile(t, cols):
            rows = pl.ds(8 * t, 8)
            return v_ref[a, rows, cols] * present(rows, cols)

        left_ref[a] = packed(lambda t: tile(t, pl.ds(0, 128)), 0, TILES // 2)
        right_ref[a] = packed(lambda t: tile(t, pl.ds(COLS - 128, 128)), 120, 0)
        return carry

    lax.fori_loop(0, VECS, vector, 0)

    def second(t, cols):
        return 0.25 * present(pl.ds(8 * t, 8), cols)

    def first(t, cols):
        return second(t, cols) * onsite_ref[pl.ds(8 * t, 8), cols]

    for k, coef in enumerate((first, second)):
        left_ref[VECS + k] = packed(lambda t: coef(t, pl.ds(0, 128)), 0, TILES // 2)
        right_ref[VECS + k] = packed(lambda t: coef(t, pl.ds(COLS - 128, 128)), 120, 0)
    for ref, t, start in ((up_ref, 0, 0), (down_ref, TILES - 1, 8 - REACH)):
        rows = pl.ds(8 * t, 8)
        block = v_ref[:, rows, :] * present(rows, slice(None))[None]
        block = jnp.swapaxes(block, 0, 1)
        for i in range(REACH):
            for h in range(2):
                ref[2 * i + h] = block[start + i, :, 128 * h : 128 * h + 128]
        for k, coef in enumerate((first, second)):
            for h in range(2):
                ref[2 * REACH + 2 * k + h] = coef(t, pl.ds(128 * h, 128))


def joined(from_left, from_right, left_slot, right_slot):
    lane = lanes(8)
    moved_left = pltpu.roll(from_left, (120 - GROUP * left_slot) % 128, 1)
    moved_right = pltpu.roll(from_right, (-GROUP * right_slot) % 128, 1)
    zero = jnp.zeros((8, 128), jnp.float32)
    return jnp.where(lane >= 120, moved_left, jnp.where(lane < GROUP, moved_right, zero))


def filter_kernel(c_ref, v0_ref, v1_ref, onsite_ref, mask_ref, vec_ref, coef_ref, out_ref, a_ref, b_ref, g_ref, d_ref, q_ref):
    half = TILES // 2
    main = slice(0, COLS)
    side = slice(COLS, WIDE)
    flats = [ref.reshape(VECS * ROWS, 128) for ref in (v0_ref, v1_ref)]

    def fill(t, carry):
        rows = pl.ds(pl.multiple_of(8 * t, 8), 8)
        second = mask_ref[rows, :].astype(jnp.float32)
        first = 0.25 * onsite_ref[rows, :]
        for i in range(8):
            present = jnp.broadcast_to(second[i : i + 1], (8, COLS))
            for h, flat in enumerate(flats):
                row = flat[pl.ds(8 * t + i, VECS, stride=ROWS), :]
                a_ref[TOP + 8 * t + i, :, 128 * h : 128 * h + 128] = row * present[:, 128 * h : 128 * h + 128]
            d_ref[TOP + 8 * t + i, :, main] = jnp.broadcast_to(first[i : i + 1], (8, COLS)) * present
            q_ref[TOP + 8 * t + i, :, main] = 0.25 * present
        return carry

    lax.fori_loop(0, TILES, fill, 0)
    west = jnp.swapaxes(vec_ref[0:8], 0, 1)
    east = jnp.swapaxes(vec_ref[8:16], 0, 1)
    for t in range(TILES):
        for i in range(8):
            a_ref[TOP + 8 * t + i, :, side] = joined(west[i], east[i], t, (t + half) % TILES)
        for k, ref in enumerate((d_ref, q_ref)):
            block = joined(coef_ref[k], coef_ref[2 + k], t, (t + half) % TILES)
            for i in range(8):
                ref[TOP + 8 * t + i, :, side] = jnp.broadcast_to(block[i : i + 1], (8, 128))
    for base, t, start, goal in ((0, TILES - 1, 8 - REACH, TOP - REACH), (1, 0, 0, TOP + ROWS)):
        at = 16 + base * (2 * REACH + 8)
        corner = jnp.swapaxes(vec_ref[at + 2 * REACH : at + 2 * REACH + 8], 0, 1)
        for i in range(REACH):
            for h in range(2):
                a_ref[goal + i, :, 128 * h : 128 * h + 128] = vec_ref[at + 2 * i + h]
            mixed = corner[start + i]
            a_ref[goal + i, :, side] = joined(mixed, mixed, t, (t + half) % TILES)
        at = 4 + base * 6
        for k, ref in enumerate((d_ref, q_ref)):
            mixed = coef_ref[at + 4 + k]
            block = joined(mixed, mixed, t, (t + half) % TILES)
            for i in range(REACH):
                for h in range(2):
                    row = coef_ref[at + 2 * k + h][start + i : start + i + 1]
                    ref[goal + i, :, 128 * h : 128 * h + 128] = jnp.broadcast_to(row, (8, 128))
                ref[goal + i, :, side] = jnp.broadcast_to(block[start + i : start + i + 1], (8, 128))
    for e in (TOP - REACH, TOP + ROWS + REACH - 1):
        b_ref[e] = jnp.zeros((VECS, WIDE), jnp.float32)
        g_ref[e] = jnp.zeros((VECS, WIDE), jnp.float32)

    even_lane = lax.broadcasted_iota(jnp.int32, (VECS, WIDE), 1) % 2 == 0

    def sweep(source, others, combine, start, count, strip=STRIP):
        def body(p, carry):
            e = start + strip * p
            rows = [source[e - 1 + k] for k in range(strip + 2)]
            coefs = [(d_ref[e + k], q_ref[e + k]) for k in range(strip)]
            loaded = [[ref[e + k] for ref in others] for k in range(strip)]
            stores = []
            for k in range(strip):
                above, centre, below = rows[k : k + 3]
                first, second = (below, above) if k % 2 == 0 else (above, below)
                near = pltpu.roll(centre, 1, 1) + pltpu.roll(centre, WIDE - 1, 1)
                near = near + jnp.where(even_lane, first, second)
                applied = coefs[k][0] * centre - coefs[k][1] * near
                stores.append((applied, centre, loaded[k]))
            combine(e, stores)
            return carry

        lax.fori_loop(0, count // strip, body, 0)

    def into(target, value):
        def combine(e, rows):
            for k, row in enumerate(rows):
                target[e + k] = value(*row)

        return combine

    c0, c1, c2, c3, c4 = (c_ref[k] for k in range(5))
    wide = ROWS + 4
    sweep(a_ref, (), into(b_ref, lambda s, x, o: c3 * x + (c4 + c4) * s), 2, wide)
    sweep(b_ref, (a_ref,), into(g_ref, lambda s, x, o: (c2 - c4) * o[0] + (s + s)), 2, wide)
    sweep(g_ref, (a_ref, b_ref), into(b_ref, lambda s, x, o: c1 * o[0] + ((s + s) - o[1])), 2, wide)
    sweep(b_ref, (a_ref, g_ref), into(g_ref, lambda s, x, o: c0 * o[0] + (s - o[1])), 2, wide)

    def finish(e, rows):
        for k, (applied, centre, _) in enumerate(rows):
            out_ref[e - TOP + k, 0:VECS, :] = centre[:, main]
            out_ref[e - TOP + k, VECS : 2 * VECS, :] = applied[:, main]

    sweep(g_ref, (), finish, TOP, ROWS, 8)


def parts_kernel(s0_ref, s1_ref, out_ref):
    count, rows, _ = s0_ref.shape
    for h, ref in enumerate((s0_ref, s1_ref)):
        flat = ref.reshape(count * rows, 128)
        cols = slice(128 * h, 128 * h + 128)
        for i in range(rows):
            block = flat[pl.ds(i, count, stride=rows), :]
            high = block.astype(jnp.bfloat16)
            out_ref[rows * pl.program_id(0) + i, 0:count, cols] = high
            out_ref[rows * pl.program_id(0) + i, count : 2 * count, cols] = (block - high.astype(jnp.float32)).astype(jnp.bfloat16)


def gram_kernel(x_ref, y_ref, s_ref, out_ref):
    def group(t, carry):
        total = None
        for k in range(16):
            r = 16 * t + k
            block = jnp.concatenate([x_ref[r], y_ref[r]], 0)
            high = block.astype(jnp.bfloat16)
            low = (block - high.astype(jnp.float32)).astype(jnp.bfloat16)
            product = lax.dot_general(
                jnp.concatenate([high, low], 0),
                s_ref[r],
                (((1,), (1,)), ((), ())),
                preferred_element_type=jnp.float32,
            )
            total = product if total is None else total + product
        return carry + total

    whole = lax.fori_loop(0, ROWS // 16, group, jnp.zeros((64, 128), jnp.float32))
    rows = whole[0:32, :] + whole[32:64, :]
    out_ref[...] = rows[:, 0:64] + rows[:, 64:128]


def floats(*shape):
    return jax.ShapeDtypeStruct(shape, jnp.float32)


def edges(block_vectors, onsite, mask):
    return pl.pallas_call(
        edges_kernel,
        name="edges",
        out_shape=tuple(floats(10, 8, 128) for _ in range(4)),
        in_specs=[VMEM] * 3,
        out_specs=(VMEM,) * 4,
        compiler_params=limit(4),
    )(block_vectors, onsite, mask)


def filtering(coefs, vectors, onsite, mask, vec_strips, coef_strips):
    return pl.pallas_call(
        filter_kernel,
        name="filtering",
        grid=(1,),
        out_shape=floats(ROWS, 2 * VECS, COLS),
        in_specs=[
            SMEM,
            pl.BlockSpec((VECS, ROWS, 128), lambda t: (0, 0, 0)),
            pl.BlockSpec((VECS, ROWS, 128), lambda t: (0, 0, 1)),
        ] + [VMEM] * 4,
        out_specs=VMEM,
        scratch_shapes=[pltpu.VMEM((EXT, VECS, WIDE), jnp.float32)] * 5,
        compiler_params=limit(18),
    )(coefs, vectors, vectors, onsite, mask, vec_strips, coef_strips)


def parts(search):
    count = search.shape[0]
    return pl.pallas_call(
        parts_kernel,
        name="parts",
        grid=(TILES,),
        out_shape=jax.ShapeDtypeStruct((ROWS, 2 * count, COLS), jnp.bfloat16),
        in_specs=[
            pl.BlockSpec((count, 8, 128), lambda t: (0, t, 0)),
            pl.BlockSpec((count, 8, 128), lambda t: (0, t, 1)),
        ],
        out_specs=VMEM,
        compiler_params=limit(12),
    )(search, search)


def gram(x, y, split):
    return pl.pallas_call(
        gram_kernel,
        name="gram",
        out_shape=floats(32, 64),
        in_specs=[VMEM] * 3,
        out_specs=VMEM,
        compiler_params=limit(20),
    )(x, y, split)


def limit(mib):
    return pltpu.CompilerParams(vmem_limit_bytes=mib << 20)


def shifted(block, axis, by):
    count = lax.axis_size(axis)
    return lax.ppermute(block, axis, [(i, i + by) for i in range(count) if 0 <= i + by < count])


def copies_sum(partial, axis):
    count = lax.axis_size(axis)
    copies = jnp.broadcast_to(partial[None], (count,) + partial.shape)
    return lax.all_to_all(copies, axis, 0, 0).sum(0)


def shards(block_vectors, search_vectors, onsite_energy, site_mask, filter_coefs):
    across = [(0, 2), (1, 3), (2, 0), (3, 1)]
    swap = [(0, 1), (1, 0), (2, 3), (3, 2)]
    left, right, up, down = edges(block_vectors, onsite_energy, site_mask)
    from_left = shifted(right, "ly", 1)
    from_right = shifted(left, "ly", -1)
    from_left, from_right, block_vectors, search_vectors = lax.optimization_barrier(
        (from_left, from_right, block_vectors, search_vectors)
    )
    far_vectors = lax.ppermute(block_vectors, "blk", across)
    slot = lax.broadcasted_iota(jnp.int32, (10, 8, 128), 2) // GROUP
    from_below = shifted(jnp.concatenate([up, jnp.where(slot == 0, from_left, from_right)], 0), "lx", -1)
    from_above = shifted(jnp.concatenate([down, jnp.where(slot == TILES - 1, from_left, from_right)], 0), "lx", 1)
    vec_strips = jnp.concatenate(
        [from_left[:8], from_right[:8]]
        + [x for f in (from_above, from_below) for x in (f[:6], f[10:18])], 0
    )
    coef_strips = jnp.concatenate(
        [from_left[8:], from_right[8:]]
        + [x for f in (from_above, from_below) for x in (f[6:10], f[18:])], 0
    )
    far_strips = lax.ppermute(vec_strips, "blk", across)
    split = parts(search_vectors)
    split, own_strips = lax.optimization_barrier((split, vec_strips))
    own = filtering(filter_coefs, block_vectors, onsite_energy, site_mask, own_strips, coef_strips)
    own_near = lax.ppermute(own, "blk", swap)
    far = filtering(filter_coefs, far_vectors, onsite_energy, site_mask, far_strips, coef_strips)
    far_near = lax.ppermute(far, "blk", swap)
    partial = jnp.concatenate([gram(own, own_near, split), gram(far, far_near, split)], 0)
    total = copies_sum(copies_sum(partial.reshape(32, 128), "ly"), "lx").reshape(4, 2, VECS, 64)
    block = lax.axis_index("blk")
    total = jnp.where(block % 2 == 1, total[jnp.array([1, 0, 3, 2])], total)
    total = jnp.where(block >= 2, total[jnp.array([2, 3, 0, 1])], total)
    nrows, ncols = onsite_energy.shape
    scale = 1.0 / math.sqrt(nrows * ncols * lax.axis_size("lx") * lax.axis_size("ly"))
    return jnp.swapaxes(total, 0, 1).reshape(2, 4 * VECS, 64) * scale


def solution(mesh):
    placed = (P("blk", "lx", "ly"), P("blk", "lx", "ly"), P("lx", "ly"), P("lx", "ly"), P())
    return jax.shard_map(
        shards, mesh=mesh, in_specs=placed, out_specs=P(None, None, "blk"), check_vma=False
    )
```

```python
import functools
import math

import jax
import jax.numpy as jnp
from jax import lax
from jax.experimental import pallas as pl
from jax.experimental.pallas import tpu as pltpu
from jax.sharding import PartitionSpec as P


VECS, ROWS, COLS = 8, 128, 256
TILES = ROWS // 8
WIDE = COLS + 128
TOP = 4
EXT = ROWS + 2 * TOP
REACH = 3
GROUP = 8
STRIP = 22
VMEM = pl.BlockSpec(memory_space=pltpu.VMEM)
HBM = pl.BlockSpec(memory_space=pltpu.HBM)
SMEM = pl.BlockSpec(memory_space=pltpu.SMEM)


def lanes(rows):
    return lax.broadcasted_iota(jnp.int32, (rows, 128), 1)


def packed(tile_of, offset, turn):
    slot = lanes(8) // GROUP
    out = jnp.zeros((8, 128), jnp.float32)
    for t in range(TILES):
        target = (t + turn) % TILES
        moved = pltpu.roll(tile_of(t), (GROUP * target - offset) % 128, 1)
        out = jnp.where(slot == target, moved, out)
    return out


def edges_kernel(
    v_hbm, onsite_hbm, mask_hbm, left_ref, right_ref, up_ref, down_ref, v_ref, onsite_ref, mask_ref, sems
):
    copies = [
        pltpu.make_async_copy(source, target, sems.at[k])
        for k, (source, target) in enumerate(
            ((v_hbm, v_ref), (onsite_hbm, onsite_ref), (mask_hbm, mask_ref))
        )
    ]
    for copy in copies:
        copy.start()
    for copy in copies:
        copy.wait()

    def present(rows, cols):
        return mask_ref[rows, cols].astype(jnp.float32)

    def vector(a, carry):
        def tile(t, cols):
            rows = pl.ds(8 * t, 8)
            return v_ref[a, rows, cols] * present(rows, cols)

        left_ref[a] = packed(lambda t: tile(t, pl.ds(0, 128)), 0, TILES // 2)
        right_ref[a] = packed(lambda t: tile(t, pl.ds(COLS - 128, 128)), 120, 0)
        return carry

    lax.fori_loop(0, VECS, vector, 0)

    def second(t, cols):
        return 0.5 * present(pl.ds(8 * t, 8), cols)

    def first(t, cols):
        return second(t, cols) * onsite_ref[pl.ds(8 * t, 8), cols]

    for k, coef in enumerate((first, second)):
        left_ref[VECS + k] = packed(lambda t: coef(t, pl.ds(0, 128)), 0, TILES // 2)
        right_ref[VECS + k] = packed(lambda t: coef(t, pl.ds(COLS - 128, 128)), 120, 0)
    for ref, t, start in ((up_ref, 0, 0), (down_ref, TILES - 1, 8 - REACH)):
        rows = pl.ds(8 * t, 8)
        block = v_ref[:, rows, :] * present(rows, slice(None))[None]
        block = jnp.swapaxes(block, 0, 1)
        for i in range(REACH):
            for h in range(2):
                ref[2 * i + h] = block[start + i, :, 128 * h : 128 * h + 128]
        for k, coef in enumerate((first, second)):
            for h in range(2):
                ref[2 * REACH + 2 * k + h] = coef(t, pl.ds(128 * h, 128))


def joined(from_left, from_right, left_slot, right_slot):
    lane = lanes(8)
    moved_left = pltpu.roll(from_left, (120 - GROUP * left_slot) % 128, 1)
    moved_right = pltpu.roll(from_right, (-GROUP * right_slot) % 128, 1)
    zero = jnp.zeros((8, 128), jnp.float32)
    return jnp.where(lane >= 120, moved_left, jnp.where(lane < GROUP, moved_right, zero))


def fill_vectors(v_refs, mask_ref, vec_ref, a_ref):
    half = TILES // 2
    side = slice(COLS, WIDE)
    flats = [ref.reshape(VECS * ROWS, 128) for ref in v_refs]

    def fill(t, carry):
        present = mask_ref[pl.ds(pl.multiple_of(8 * t, 8), 8), :].astype(jnp.float32)
        for i in range(8):
            for h, flat in enumerate(flats):
                row = flat[pl.ds(8 * t + i, VECS, stride=ROWS), :]
                kept = jnp.broadcast_to(present[i : i + 1, 128 * h : 128 * h + 128], (8, 128))
                a_ref[TOP + 8 * t + i, :, 128 * h : 128 * h + 128] = row * kept
        return carry

    lax.fori_loop(0, TILES, fill, 0)
    west = jnp.swapaxes(vec_ref[0:8], 0, 1)
    east = jnp.swapaxes(vec_ref[8:16], 0, 1)
    for t in range(TILES):
        for i in range(8):
            a_ref[TOP + 8 * t + i, :, side] = joined(west[i], east[i], t, (t + half) % TILES)
    for base, t, start, goal in ((0, TILES - 1, 8 - REACH, TOP - REACH), (1, 0, 0, TOP + ROWS)):
        at = 16 + base * (2 * REACH + 8)
        corner = jnp.swapaxes(vec_ref[at + 2 * REACH : at + 2 * REACH + 8], 0, 1)
        for i in range(REACH):
            for h in range(2):
                a_ref[goal + i, :, 128 * h : 128 * h + 128] = vec_ref[at + 2 * i + h]
            mixed = corner[start + i]
            a_ref[goal + i, :, side] = joined(mixed, mixed, t, (t + half) % TILES)


def fill_coefs(onsite_ref, mask_ref, coef_ref, d_ref, q_ref):
    half = TILES // 2
    main = slice(0, COLS)
    side = slice(COLS, WIDE)

    def fill(t, carry):
        rows = pl.ds(pl.multiple_of(8 * t, 8), 8)
        second = 0.5 * mask_ref[rows, :].astype(jnp.float32)
        first = second * onsite_ref[rows, :]
        for i in range(8):
            d_ref[TOP + 8 * t + i, :, main] = jnp.broadcast_to(first[i : i + 1], (8, COLS))
            q_ref[TOP + 8 * t + i, :, main] = jnp.broadcast_to(second[i : i + 1], (8, COLS))
        return carry

    lax.fori_loop(0, TILES, fill, 0)
    for t in range(TILES):
        for k, ref in enumerate((d_ref, q_ref)):
            block = joined(coef_ref[k], coef_ref[2 + k], t, (t + half) % TILES)
            for i in range(8):
                ref[TOP + 8 * t + i, :, side] = jnp.broadcast_to(block[i : i + 1], (8, 128))
    for base, t, start, goal in ((0, TILES - 1, 8 - REACH, TOP - REACH), (1, 0, 0, TOP + ROWS)):
        at = 4 + base * 6
        for k, ref in enumerate((d_ref, q_ref)):
            mixed = coef_ref[at + 4 + k]
            block = joined(mixed, mixed, t, (t + half) % TILES)
            for i in range(REACH):
                for h in range(2):
                    row = coef_ref[at + 2 * k + h][start + i : start + i + 1]
                    ref[goal + i, :, 128 * h : 128 * h + 128] = jnp.broadcast_to(row, (8, 128))
                ref[goal + i, :, side] = jnp.broadcast_to(block[start + i : start + i + 1], (8, 128))


def own_kernel(c_ref, v0_ref, v1_ref, onsite_ref, mask_ref, vec_ref, coef_ref, out_ref, d_ref, q_ref, *scratch):
    fill_coefs(onsite_ref, mask_ref, coef_ref, d_ref, q_ref)
    fill_vectors((v0_ref, v1_ref), mask_ref, vec_ref, scratch[0])
    sweeps(c_ref, d_ref, q_ref, out_ref, *scratch)


def far_kernel(c_ref, v0_ref, v1_ref, mask_ref, vec_ref, d_ref, q_ref, out_ref, *scratch):
    fill_vectors((v0_ref, v1_ref), mask_ref, vec_ref, scratch[0])
    sweeps(c_ref, d_ref, q_ref, out_ref, *scratch)


def sweeps(c_ref, d_ref, q_ref, out_ref, a_ref, b_ref, g_ref):
    main = slice(0, COLS)
    for e in (TOP - REACH, TOP + ROWS + REACH - 1):
        b_ref[e] = jnp.zeros((VECS, WIDE), jnp.float32)
        g_ref[e] = jnp.zeros((VECS, WIDE), jnp.float32)
    even_lane = lax.broadcasted_iota(jnp.int32, (VECS, WIDE), 1) % 2 == 0

    def sweep(source, others, combine, start, count, strip):
        def body(p, carry):
            e = start + strip * p
            rows = [source[e - 1 + k] for k in range(strip + 2)]
            coefs = [(d_ref[e + k], q_ref[e + k]) for k in range(strip)]
            loaded = [[ref[e + k] for ref in others] for k in range(strip)]
            stores = []
            for k in range(strip):
                above, centre, below = rows[k : k + 3]
                first, second = (below, above) if k % 2 == 0 else (above, below)
                near = pltpu.roll(centre, 1, 1) + pltpu.roll(centre, WIDE - 1, 1)
                near = near + jnp.where(even_lane, first, second)
                twice = coefs[k][0] * centre - coefs[k][1] * near
                stores.append((twice, centre, loaded[k]))
            combine(e, stores)
            return carry

        lax.fori_loop(0, count // strip, body, 0)

    def into(target, value):
        def combine(e, rows):
            for k, row in enumerate(rows):
                target[e + k] = value(*row)

        return combine

    c0, c1, c2, c3, c4 = (c_ref[k] for k in range(5))
    wide = ROWS + 4
    sweep(a_ref, (), into(b_ref, lambda s, x, o: c3 * x + c4 * s), 2, wide, STRIP)
    sweep(b_ref, (a_ref,), into(g_ref, lambda s, x, o: (c2 - c4) * o[0] + s), 2, wide, STRIP)
    sweep(g_ref, (a_ref, b_ref), into(b_ref, lambda s, x, o: c1 * o[0] + (s - o[1])), 2, wide, STRIP)
    sweep(b_ref, (a_ref, g_ref), into(g_ref, lambda s, x, o: c0 * o[0] + (0.5 * s - o[1])), 2, wide, STRIP)

    def finish(e, rows):
        for k, (twice, centre, _) in enumerate(rows):
            out_ref[e - TOP + k, 0:VECS, :] = centre[:, main]
            out_ref[e - TOP + k, VECS : 2 * VECS, :] = twice[:, main]

    sweep(g_ref, (), finish, TOP, ROWS, 16)


def parts_kernel(first, s_hbm, out_ref, buffer, sems):
    count = s_hbm.shape[0]
    rows = ROWS // 2
    copies = [
        pltpu.make_async_copy(
            s_hbm.at[:, pl.ds(first + 8 * t, 8), pl.ds(128 * h, 128)],
            buffer.at[h, :, pl.ds(8 * t, 8), :],
            sems.at[t, h],
        )
        for t in range(rows // 8)
        for h in range(2)
    ]
    for copy in copies:
        copy.start()
    flat = buffer.reshape(2 * count * rows, 128)
    for t in range(rows // 8):
        copies[2 * t].wait()
        copies[2 * t + 1].wait()

        def split(i, carry):
            for h in range(2):
                cols = slice(128 * h, 128 * h + 128)
                r = 8 * t + i
                block = flat[pl.ds(h * count * rows + r, count, stride=rows), :]
                high = block.astype(jnp.bfloat16)
                out_ref[r, 0:count, cols] = high
                out_ref[r, count : 2 * count, cols] = (block - high.astype(jnp.float32)).astype(jnp.bfloat16)
            return carry

        lax.fori_loop(0, 8, split, 0, unroll=4)


def product(x_ref, y_ref, s_refs):
    def group(s_ref, first):
        def body(t, carry):
            total = None
            for k in range(16):
                r = 16 * t + k
                block = jnp.concatenate([x_ref[first + r], y_ref[first + r]], 0)
                high = block.astype(jnp.bfloat16)
                low = (block - high.astype(jnp.float32)).astype(jnp.bfloat16)
                one = lax.dot_general(
                    jnp.concatenate([high, low], 0),
                    s_ref[r],
                    (((1,), (1,)), ((), ())),
                    preferred_element_type=jnp.float32,
                )
                total = one if total is None else total + one
            return carry + total

        return body

    whole = jnp.zeros((64, 128), jnp.float32)
    for k, s_ref in enumerate(s_refs):
        whole = lax.fori_loop(0, ROWS // 32, group(s_ref, k * ROWS // 2), whole)
    rows = whole[0:32, :] + whole[32:64, :]
    return rows[:, 0:64] + rows[:, 64:128]


def first_gram_kernel(x_ref, y_ref, s0_ref, s1_ref, out_ref):
    out_ref[...] = product(x_ref, y_ref, (s0_ref, s1_ref))


def second_gram_kernel(x_ref, y_ref, s0_ref, s1_ref, other_ref, out_ref):
    both = jnp.concatenate([other_ref[...], product(x_ref, y_ref, (s0_ref, s1_ref))], 1)
    for k in range(out_ref.shape[0]):
        out_ref[k] = both


def spread_kernel(x_ref, out_ref):
    total = jnp.sum(x_ref[...], 0)
    for k in range(out_ref.shape[0]):
        out_ref[k] = total


def finish_kernel(scale, x_ref, out_ref):
    own = lax.axis_index("blk")
    total = jnp.sum(x_ref[...], 0)
    for k in range(4):
        block = own ^ k
        cols = slice(64 * (k // 2), 64 * (k // 2) + 64)
        for s in range(2):
            rows = 16 * (k % 2) + 8 * s
            value = total[rows : rows + 8, cols] * (scale if s == 0 else 0.5 * scale)
            out_ref[s, pl.ds(pl.multiple_of(8 * block, 8), 8), :] = value


def floats(*shape):
    return jax.ShapeDtypeStruct(shape, jnp.float32)


def edges(block_vectors, onsite, mask):
    return pl.pallas_call(
        edges_kernel,
        name="edges",
        out_shape=tuple(floats(10, 8, 128) for _ in range(4)),
        in_specs=[HBM] * 3,
        out_specs=(VMEM,) * 4,
        scratch_shapes=[
            pltpu.VMEM((VECS, ROWS, COLS), jnp.float32),
            pltpu.VMEM((ROWS, COLS), jnp.float32),
            pltpu.VMEM((ROWS, COLS), jnp.int32),
            pltpu.SemaphoreType.DMA((3,)),
        ],
        compiler_params=limit(4),
    )(*(pltpu.with_memory_space_constraint(x, pltpu.HBM) for x in (block_vectors, onsite, mask)))


def filtering(coefs, vectors, mask, vec_strips, onsite=None, coef_strips=None, prepared=None):
    own = prepared is None
    wide = (EXT, VECS, WIDE)
    result = floats(ROWS, 2 * VECS, COLS)
    vector_specs = [
        SMEM,
        pl.BlockSpec((VECS, ROWS, 128), lambda t: (0, 0, 0)),
        pl.BlockSpec((VECS, ROWS, 128), lambda t: (0, 0, 1)),
    ]
    if own:
        operands = (coefs, vectors, vectors, onsite, mask, vec_strips, coef_strips)
    else:
        operands = (coefs, vectors, vectors, mask, vec_strips) + tuple(prepared)
    return pl.pallas_call(
        own_kernel if own else far_kernel,
        name="own" if own else "far",
        grid=(1,),
        out_shape=(result, floats(*wide), floats(*wide)) if own else result,
        in_specs=vector_specs + [VMEM] * 4,
        out_specs=(VMEM,) * 3 if own else VMEM,
        scratch_shapes=[pltpu.VMEM(wide, jnp.float32)] * 3,
        compiler_params=limit(18),
    )(*operands)


def parts(search, half):
    count = search.shape[0]
    rows = ROWS // 2
    return pl.pallas_call(
        functools.partial(parts_kernel, half * rows),
        name="parts",
        out_shape=jax.ShapeDtypeStruct((rows, 2 * count, COLS), jnp.bfloat16),
        in_specs=[HBM],
        out_specs=VMEM,
        scratch_shapes=[
            pltpu.VMEM((2, count, rows, 128), jnp.float32),
            pltpu.SemaphoreType.DMA((rows // 8, 2)),
        ],
        compiler_params=limit(10),
    )(pltpu.with_memory_space_constraint(search, pltpu.HBM))


def small(kernel, shape, limited, *operands):
    return pl.pallas_call(
        kernel,
        out_shape=floats(*shape),
        in_specs=[VMEM] * len(operands),
        out_specs=VMEM,
        compiler_params=limit(limited),
    )(*operands)


def limit(mib):
    return pltpu.CompilerParams(vmem_limit_bytes=mib << 20)


def shifted(block, axis, by):
    count = lax.axis_size(axis)
    return lax.ppermute(block, axis, [(i, i + by) for i in range(count) if 0 <= i + by < count])


def strips(above_below, picks):
    return [f[low:high] for f in above_below for low, high in picks]


def program(block_vectors, search_vectors, onsite_energy, site_mask, filter_coefs):
    across = [(0, 2), (1, 3), (2, 0), (3, 1)]
    swap = [(0, 1), (1, 0), (2, 3), (3, 2)]
    left, right, up, down = edges(block_vectors, onsite_energy, site_mask)
    from_left = shifted(right, "ly", 1)
    from_right = shifted(left, "ly", -1)
    far_vectors = lax.ppermute(block_vectors, "blk", across)
    split_low = parts(search_vectors, 0)
    slot = lax.broadcasted_iota(jnp.int32, (10, 8, 128), 2) // GROUP
    up = jnp.concatenate([up, jnp.where(slot == 0, from_left, from_right)], 0)
    from_below = shifted(up, "lx", -1)
    down = jnp.concatenate([down, jnp.where(slot == TILES - 1, from_left, from_right)], 0)
    from_above = shifted(down, "lx", 1)
    split_high = parts(search_vectors, 1)
    outer = (from_above, from_below)
    vec_strips = jnp.concatenate([from_left[:8], from_right[:8]] + strips(outer, ((0, 6), (10, 18))), 0)
    coef_strips = jnp.concatenate([from_left[8:], from_right[8:]] + strips(outer, ((6, 10), (18, 20))), 0)
    far_strips = lax.ppermute(vec_strips, "blk", across)
    own, *prepared = filtering(
        filter_coefs, block_vectors, site_mask, vec_strips, onsite_energy, coef_strips
    )
    own_near = lax.ppermute(own, "blk", swap)
    far = filtering(filter_coefs, far_vectors, site_mask, far_strips, prepared=prepared)
    far_near = lax.ppermute(far, "blk", swap)
    first = small(first_gram_kernel, (32, 64), 20, own, own_near, split_low, split_high)
    count = lax.axis_size("ly")
    copies = small(second_gram_kernel, (count, 32, 128), 20, far, far_near, split_low, split_high, first)
    copies = lax.all_to_all(copies, "ly", 0, 0)
    copies = small(spread_kernel, (lax.axis_size("lx"), 32, 128), 2, copies)
    copies = lax.all_to_all(copies, "lx", 0, 0)
    nrows, ncols = onsite_energy.shape
    scale = 1.0 / math.sqrt(nrows * ncols * lax.axis_size("lx") * lax.axis_size("ly"))
    return small(functools.partial(finish_kernel, scale), (2, 4 * VECS, 64), 2, copies)


def solution(mesh):
    placed = (P("blk", "lx", "ly"), P("blk", "lx", "ly"), P("lx", "ly"), P("lx", "ly"), P())
    return jax.shard_map(program, mesh=mesh, in_specs=placed, out_specs=P(None, None, "blk"), check_vma=False)
```
